128 devices in a mesh: sample: 4 (over y_hi, core), turb: 32 (over x, y_lo, z).
Axes of the slice: x: 4, y: 4 (y_hi: 2, y_lo: 2; y = y_hi * 2 + y_lo), z: 4, core: 2. Of those that a mesh axis runs over, the one named last changes fastest.
Arguments:
- inflow: bfloat16 [32, 4096, 512], P('sample', 'turb'), may hold values from -6 to 6
- cotangent: bfloat16 [32, 4096, 512], P('sample', 'turb'), may hold values from -6 to 6
- norm_gain: float32 [512], replicated, may hold values from 0.25 to 1.75
- query_weight: bfloat16 [512, 512], replicated, may hold values from -2 to 2, as said below
- key_weight: bfloat16 [512, 512], replicated, may hold values from -2 to 2, as said below
- value_weight: bfloat16 [512, 512], replicated, may hold values from -0.25 to 0.25
- out_weight: bfloat16 [512, 512], replicated, may hold values from -0.25 to 0.25
- adjacency: int32 [8, 32, 3], replicated, may hold values from -1 to 31, as said below
- sectors: int32 [32], P('sample'), may hold values from 0 to 7, as said below
Outputs:
- layer_output: bfloat16 [32, 4096, 512], P('sample', 'turb')
- grad_inflow: bfloat16 [32, 4096, 512], P('sample', 'turb')
- grad_query_weight: float32 [512, 512], replicated
- grad_key_weight: float32 [512, 512], replicated
- grad_value_weight: float32 [512, 512], replicated
- grad_out_weight: float32 [512, 512], replicated
- grad_norm_gain: float32 [512], replicated
The draws below stay inside these ranges and needn't reach their ends.
Inputs may be any that keep to these rules, and one draw needn't show every extreme that they name: `adjacency`: row [s, b] lists distinct blocks other than b, the used entries first and -1 after them. For every block and every group of 8 consecutive samples, another block is listed upstream of it for at most 1 of the group's samples, and some pair of blocks reaches 1. `sectors`: every group of 8 consecutive samples holds each sector exactly 1 times. `query_weight`: A projection of rows of 512 features. `key_weight`: A projection of rows of 512 features.
All inputs are finite; a program needn't handle non-finite values.
Results may differ from the reference program's by a relative error of at most 0.004.
The reference program's roundings to bfloat16 on the way count: a program that leaves them out, or rounds other values in their place, can miss the bound.
Values may be sent and summed in bfloat16 or wider, within the bound.
A program may use at most 192 MiB of HBM per device.

```python
import math
import jax
import jax.numpy as jnp
from jax import lax

D = 512
HEADS = 8
BLOCK = 128
UPSTREAM = 3
SECTORS = 8
SAMP_DEV = 8
SAMPLES = 32
BLOCKS = 32
TURBINES = 4096


def draw_adjacency(key, part):
    base = jax.random.fold_in(key, 101)
    order_key, count_key, pick_key = jax.random.split(base, 3)
    others = BLOCKS - 1
    orders = jax.vmap(lambda single: jax.random.permutation(single, others))(jax.random.split(order_key, BLOCKS))
    block_ids = jnp.arange(BLOCKS, dtype=jnp.int32)
    sources = (block_ids[:, None] + 1 + orders.astype(jnp.int32)) % BLOCKS
    counts = jax.random.randint(count_key, (SECTORS, BLOCKS), 0, UPSTREAM + 1)
    fullest = jax.random.randint(pick_key, (), 0, BLOCKS)
    counts = jnp.where(block_ids[None, :] == fullest, UPSTREAM, counts)
    slot_ids = jnp.arange(UPSTREAM, dtype=jnp.int32)
    places = (jnp.arange(SECTORS, dtype=jnp.int32)[:, None] * UPSTREAM + slot_ids[None, :]) % others
    picked = jnp.transpose(sources[:, places], (1, 0, 2))
    return jnp.where(slot_ids[None, None, :] < counts[:, :, None], picked, -1).astype(jnp.int32)


def draw_sectors(key, part):
    base = jax.random.fold_in(key, 202)
    groups = SAMPLES // SAMP_DEV
    orders = jax.vmap(lambda single: jax.random.permutation(single, SAMP_DEV))(jax.random.split(base, groups))
    return (orders.astype(jnp.int32) % SECTORS).reshape(SAMPLES)


def draw_query_weight(key, part):
    single = jax.random.normal(jax.random.fold_in(key, 1), (D, D), jnp.float32) / math.sqrt(D)
    return jnp.clip(single, -2.0, 2.0).astype(jnp.bfloat16)


def draw_key_weight(key, part):
    single = jax.random.normal(jax.random.fold_in(key, 2), (D, D), jnp.float32) / math.sqrt(D)
    return jnp.clip(single, -2.0, 2.0).astype(jnp.bfloat16)


def block_levels(rng, shape, shards, low, high):
    def one(position, shards_of):
        heights = jax.random.uniform(jax.random.fold_in(jax.random.fold_in(rng, 6), position), (shards_of,), jnp.float32, low / len(shards), high / len(shards))
        return jnp.repeat(jnp.exp(heights), shape[position] // shards_of).reshape((-1,) + (1,) * (len(shape) - position - 1))

    gain = one(*shards[0])
    for cut in shards[1:]:
        gain = gain * one(*cut)
    return gain


def scatter_about(own_key, shape, spread, most, cuts=(), held_as=jnp.bfloat16):
    entries = jax.random.normal(own_key, shape, jnp.float32) * spread
    if len(cuts) > 0:
        entries = block_levels(own_key, shape, cuts, -0.22, 0.18) * entries
    return jnp.clip(entries, min=-most, max=most).astype(held_as)


def setup_inputs(seed: int = 0) -> dict:
    arg_keys = jax.random.split(jax.random.key(seed), 10)
    return {
        "inflow": scatter_about(arg_keys[0], (SAMPLES, TURBINES, D), 1.0, 6.0, ((0, 4), (1, 32))),
        "cotangent": scatter_about(arg_keys[1], (SAMPLES, TURBINES, D), 1.0, 6.0, ((0, 4), (1, 32))),
        "norm_gain": jnp.clip(1.0 + 0.15 * jax.random.normal(arg_keys[2], (D,), jnp.float32), 0.25, 1.75),
        "query_weight": draw_query_weight(jax.random.fold_in(arg_keys[9], 71), 0),
        "key_weight": draw_key_weight(jax.random.fold_in(arg_keys[9], 71), 0),
        "value_weight": scatter_about(arg_keys[5], (D, D), D ** -0.5, 0.25),
        "out_weight": scatter_about(arg_keys[6], (D, D), D ** -0.5, 0.25),
        "adjacency": draw_adjacency(jax.random.fold_in(arg_keys[9], 71), 0),
        "sectors": draw_sectors(jax.random.fold_in(arg_keys[9], 71), 0),
    }


epsilon = 1e-05

def normalize(row_block, norm_gain):
    widened = row_block.astype(jnp.float32)
    centred = widened - lax.optimization_barrier(jnp.mean(widened, axis=-1, keepdims=True))
    inverse = lax.rsqrt(lax.optimization_barrier(jnp.mean(centred * centred, axis=-1, keepdims=True)) + epsilon)
    scaled = centred * inverse
    return (scaled, inverse, (scaled * norm_gain).astype(jnp.bfloat16))

def attend(queries, key_rows, value_rows, key_usable, grad_attended):
    batch_count, query_count, model_width = queries.shape
    key_count = key_rows.shape[1]
    head_dim = model_width // HEADS
    score_scale = head_dim ** (-0.5)
    query_heads = queries.reshape(batch_count, query_count, HEADS, head_dim).astype(jnp.float32)
    key_heads = key_rows.reshape(batch_count, key_count, HEADS, head_dim).astype(jnp.float32)
    value_heads = value_rows.reshape(batch_count, key_count, HEADS, head_dim).astype(jnp.float32)
    grad_heads = grad_attended.reshape(batch_count, query_count, HEADS, head_dim).astype(jnp.float32)
    scores = jnp.einsum('nqhd,nkhd->nhqk', query_heads, key_heads) * score_scale
    scores = jnp.where(key_usable[:, None, None, :], scores, -1e+30)
    highest = lax.optimization_barrier(jnp.max(scores, axis=-1, keepdims=True))
    weights = jnp.exp(scores - highest)
    probabilities = weights / lax.optimization_barrier(jnp.sum(weights, axis=-1, keepdims=True))
    rounded = probabilities.astype(jnp.bfloat16)
    attended = jnp.einsum('nhqk,nkhd->nqhd', rounded.astype(jnp.float32), value_heads).astype(jnp.bfloat16)
    grad_probs = jnp.einsum('nqhd,nkhd->nhqk', grad_heads, value_heads)
    centred = grad_probs - lax.optimization_barrier(jnp.sum(probabilities * grad_probs, axis=-1, keepdims=True))
    grad_scores = (probabilities * centred * score_scale).astype(jnp.bfloat16)
    grad_queries = jnp.einsum('nhqk,nkhd->nqhd', grad_scores.astype(jnp.float32), key_heads).astype(jnp.bfloat16)
    grad_keys = jnp.einsum('nhqk,nqhd->nkhd', grad_scores.astype(jnp.float32), query_heads)
    grad_values = jnp.einsum('nhqk,nqhd->nkhd', rounded.astype(jnp.float32), grad_heads)
    pair_terms = jnp.concatenate([grad_keys.reshape(batch_count, key_count, model_width), grad_values.reshape(batch_count, key_count, model_width)], axis=-1)
    return (attended.reshape(batch_count, query_count, model_width), grad_queries.reshape(batch_count, query_count, model_width), pair_terms)

def reference(inflow, cotangent, norm_gain, query_weight, key_weight, value_weight, out_weight, adjacency, sectors):

    def one_sample(totals, pieces):
        input_rows, grad_rows, sector = pieces
        scaled, inverse, normed = normalize(input_rows, norm_gain)
        queries = jnp.dot(normed, query_weight, preferred_element_type=jnp.float32).astype(jnp.bfloat16)
        key_rows = jnp.dot(normed, key_weight, preferred_element_type=jnp.float32).astype(jnp.bfloat16)
        value_rows = jnp.dot(normed, value_weight, preferred_element_type=jnp.float32).astype(jnp.bfloat16)
        upstream = adjacency[sector]
        usable = upstream >= 0
        safe_lists = jnp.where(usable, upstream, 0)
        key_blocks = key_rows.reshape(BLOCKS, BLOCK, D)
        value_blocks = value_rows.reshape(BLOCKS, BLOCK, D)
        key_all = jnp.concatenate([key_blocks[:, None], key_blocks[safe_lists]], axis=1).reshape(BLOCKS, (1 + UPSTREAM) * BLOCK, D)
        value_all = jnp.concatenate([value_blocks[:, None], value_blocks[safe_lists]], axis=1).reshape(BLOCKS, (1 + UPSTREAM) * BLOCK, D)
        block_usable = jnp.concatenate([jnp.ones((BLOCKS, 1), dtype=jnp.bool_), usable], axis=1)
        key_usable = jnp.repeat(block_usable, BLOCK, axis=1)
        grad_attended = jnp.dot(grad_rows, out_weight.T, preferred_element_type=jnp.float32).astype(jnp.bfloat16)
        attended, grad_queries, pair_terms = attend(queries.reshape(BLOCKS, BLOCK, D), key_all, value_all, key_usable, grad_attended.reshape(BLOCKS, BLOCK, D))
        attended = attended.reshape(TURBINES, D)
        grad_queries = grad_queries.reshape(TURBINES, D)
        layer_output = (input_rows.astype(jnp.float32) + jnp.dot(attended, out_weight, preferred_element_type=jnp.float32)).astype(jnp.bfloat16)
        pair_terms = pair_terms.reshape(BLOCKS, 1 + UPSTREAM, BLOCK, 2 * D)
        sent_terms = lax.optimization_barrier(pair_terms[:, 1:].astype(jnp.bfloat16)).astype(jnp.float32)
        target = jnp.where(usable, upstream, BLOCKS).reshape(-1)
        combined = pair_terms[:, 0].at[target].add(sent_terms.reshape(BLOCKS * UPSTREAM, BLOCK, 2 * D), mode='drop')
        combined = combined.astype(jnp.bfloat16).reshape(TURBINES, 2 * D)
        grad_keys = combined[:, :D]
        grad_values = combined[:, D:]
        sum_query = jnp.dot(normed.T, grad_queries, preferred_element_type=jnp.float32)
        sum_key = jnp.dot(normed.T, grad_keys, preferred_element_type=jnp.float32)
        sum_value = jnp.dot(normed.T, grad_values, preferred_element_type=jnp.float32)
        sum_out = jnp.dot(attended.T, grad_rows, preferred_element_type=jnp.float32)
        grad_normed = jnp.dot(grad_queries, query_weight.T, preferred_element_type=jnp.float32)
        grad_normed = grad_normed + jnp.dot(grad_keys, key_weight.T, preferred_element_type=jnp.float32)
        grad_normed = grad_normed + jnp.dot(grad_values, value_weight.T, preferred_element_type=jnp.float32)
        sum_gain = lax.optimization_barrier(jnp.sum(grad_normed * scaled, axis=0))
        grad_scaled = grad_normed * norm_gain
        grad_input = inverse * (grad_scaled - lax.optimization_barrier(jnp.mean(grad_scaled, axis=-1, keepdims=True)) - scaled * lax.optimization_barrier(jnp.mean(grad_scaled * scaled, axis=-1, keepdims=True)))
        grad_inflow = (grad_rows.astype(jnp.float32) + grad_input).astype(jnp.bfloat16)
        new_totals = (totals[0] + sum_query, totals[1] + sum_key, totals[2] + sum_value, totals[3] + sum_out, totals[4] + sum_gain)
        return (new_totals, (layer_output, grad_inflow))
    zero_square = jnp.zeros((D, D), jnp.float32)
    start = (zero_square, zero_square, zero_square, zero_square, jnp.zeros((D,), jnp.float32))
    totals, outputs = lax.scan(one_sample, start, (inflow, cotangent, sectors))
    return (outputs[0], outputs[1], totals[0], totals[1], totals[2], totals[3], totals[4])
```

```python
import jax
import jax.numpy as jnp
from jax import lax
from jax.experimental import pallas as pl
from jax.experimental.pallas import tpu as pltpu
from jax.sharding import PartitionSpec as P

F32 = jnp.float32
BF16 = jnp.bfloat16
HEADS = 8
UPSTREAM = 3
EPSILON = 1e-05
VMEM_BYTES = 56 << 20


def dot(a, b):
    return jnp.dot(a, b, preferred_element_type=F32)


def dot_nt(a, b):
    return lax.dot_general(a, b, (((1,), (1,)), ((), ())), preferred_element_type=F32)


def whole(*shape):
    return pl.BlockSpec(shape, lambda *_: (0,) * len(shape))


def row_statistics(rows):
    widened = rows.astype(F32)
    centred = widened - jnp.mean(widened, axis=-1, keepdims=True)
    inverse = lax.rsqrt(jnp.mean(centred * centred, axis=-1, keepdims=True) + EPSILON)
    return centred * inverse, inverse


def normalize_and_pack(chosen_ref, inflow_ref, gain_ref, normed_ref, packed_ref):
    for s in range(inflow_ref.shape[0]):
        scaled, _ = row_statistics(inflow_ref[s])
        normed_ref[s] = (scaled * gain_ref[...]).astype(BF16)

    @pl.loop(0, packed_ref.shape[0])
    def _(d):
        packed_ref[d] = normed_ref[chosen_ref[d]]


def attend(
    order_ref,
    source_ref,
    target_ref,
    count_ref,
    own_ref,
    inflow_ref,
    cotangent_ref,
    up0_ref,
    up1_ref,
    up2_ref,
    wq_ref,
    wkv_ref,
    wkv_t_ref,
    wq_t_ref,
    wo_ref,
    wo_t_ref,
    out_ref,
    grad_own_ref,
    sent_ref,
    gw_ref,
    x_ref,
    kv_ref,
    kvt_ref,
    dkv_ref,
    att_t_ref,
    dq_t_ref,
):
    step = pl.program_id(0)
    block, width = own_ref.shape[1], own_ref.shape[2]
    pair = 2 * (width // HEADS)
    used = count_ref[step]

    @pl.when(step == 0)
    def _():
        gw_ref[...] = jnp.zeros_like(gw_ref)

    own = own_ref[0]
    cot = cotangent_ref[0]
    x_ref[0:block] = own
    for u, ref in enumerate((up0_ref, up1_ref, up2_ref)):
        x_ref[(u + 1) * block : (u + 2) * block] = ref[0]
    x = x_ref[...]
    kv_ref[...] = dot(x, wkv_ref[...]).astype(BF16)
    kvt_ref[...] = dot_nt(wkv_t_ref[...], x).astype(BF16)
    queries = (dot(own, wq_ref[...]).astype(BF16).astype(F32) * 0.125).astype(BF16)
    grads = dot(cot, wo_t_ref[...]).astype(BF16)
    lane = lax.broadcasted_iota(jnp.int32, (block, pair), 1) < pair // 2
    sub = lax.broadcasted_iota(jnp.int32, (pair, block), 0) < pair // 2
    zero = jnp.zeros((block, pair), BF16)
    bias = [jnp.where(u < used, 0.0, -1e30).astype(F32) for u in range(UPSTREAM)]

    def spread(rows):
        return jnp.concatenate([jnp.where(lane, rows, zero), jnp.where(lane, zero, rows)], axis=0)

    for p in range(width // pair):
        lo, hi = p * pair, (p + 1) * pair
        q_pair = spread(queries[:, lo:hi])
        g_pair = spread(grads[:, lo:hi])
        scores = dot_nt(kv_ref[:, lo:hi], q_pair)
        scores = jnp.concatenate(
            [scores[0:block]]
            + [scores[(u + 1) * block : (u + 2) * block] + bias[u] for u in range(UPSTREAM)],
            axis=0,
        )
        highest = jnp.max(scores, axis=0, keepdims=True)
        weights = jnp.exp(scores - highest)
        probs = weights * (1.0 / jnp.sum(weights, axis=0, keepdims=True))
        rounded = probs.astype(BF16)
        grad_probs = dot_nt(kv_ref[:, width + lo : width + hi], g_pair)
        centre = jnp.sum(probs * grad_probs, axis=0, keepdims=True)
        grad_scores = (probs * (grad_probs - centre)).astype(BF16)
        dkv_ref[:, width + lo : width + hi] = dot(rounded, g_pair).astype(BF16)
        dkv_ref[:, lo:hi] = dot(grad_scores, q_pair).astype(BF16)
        both = dot(kvt_ref[width + lo : width + hi, :], rounded)
        att_t_ref[lo:hi, :] = jnp.where(sub, both[:, :block], both[:, block:]).astype(BF16)
        both = dot(kvt_ref[lo:hi, :], grad_scores) * 0.125
        dq_t_ref[lo:hi, :] = jnp.where(sub, both[:, :block], both[:, block:]).astype(BF16)

    attended = att_t_ref[...].T
    dq = dq_t_ref[...].T
    out_ref[0] = (inflow_ref[0].astype(F32) + dot(attended, wo_ref[...])).astype(BF16)
    back = dot(dkv_ref[...], wkv_t_ref[...])
    grad_own_ref[0] = back[0:block] + dot(dq, wq_t_ref[...])
    for u in range(UPSTREAM):
        sent_ref[target_ref[UPSTREAM * step + u]] = back[
            (u + 1) * block : (u + 2) * block
        ].astype(BF16)
    x_t = x.T
    gw_ref[0] += dot(x_t[:, 0:block], dq)
    gw_kv = dot(x_t, dkv_ref[...])
    gw_ref[1] += gw_kv[:, :width]
    gw_ref[2] += gw_kv[:, width:]
    gw_ref[3] += dot(att_t_ref[...], cot)


def finish(
    chosen_ref, wanted_ref, grad_own_ref, returned_ref, inflow_ref, cotangent_ref, gain_ref, out_ref, sum_ref
):
    sum_ref[...] = grad_own_ref[...]

    @pl.loop(0, returned_ref.shape[0])
    def _(d):
        @pl.when(wanted_ref[d] > 0)
        def _():
            s = chosen_ref[d]
            sum_ref[s] = sum_ref[s] + returned_ref[d].astype(F32)

    for s in range(inflow_ref.shape[0]):
        scaled, inverse = row_statistics(inflow_ref[s])
        grad_scaled = sum_ref[s] * gain_ref[...]
        grad_input = inverse * (
            grad_scaled
            - jnp.mean(grad_scaled, axis=-1, keepdims=True)
            - scaled * jnp.mean(grad_scaled * scaled, axis=-1, keepdims=True)
        )
        out_ref[s] = (cotangent_ref[s].astype(F32) + grad_input).astype(BF16)


def on_device(
    inflow, cotangent, norm_gain, query_weight, key_weight, value_weight, out_weight, adjacency, sectors
):
    samples, block, width = inflow.shape
    blocks = lax.axis_size("turb")
    me = lax.axis_index("turb")
    gain = norm_gain.reshape(1, width)
    sample_ids = lax.broadcasted_iota(jnp.int32, (samples, samples), 0)
    sector_ids = lax.broadcasted_iota(jnp.int32, (samples, samples), 1)
    order = jnp.sum(jnp.where(sectors[:, None] == sector_ids, sample_ids, 0), axis=0)
    lists_me = adjacency == me
    chosen = jnp.sum(jnp.where(lists_me, order[:, None, None], 0), axis=(0, 2))
    wanted = jnp.sum(lists_me.astype(jnp.int32), axis=(0, 2))
    own_lists = lax.dynamic_index_in_dim(adjacency, me, axis=1, keepdims=False)
    usable = own_lists >= 0
    count = jnp.sum(usable.astype(jnp.int32), axis=1)
    spare = jnp.where(me == 0, 1, 0)
    source = jnp.where(usable, own_lists, spare).reshape(-1)
    target = jnp.where(usable, own_lists, me).reshape(-1)

    rows = jax.ShapeDtypeStruct((samples, block, width), BF16)
    buffer = jax.ShapeDtypeStruct((blocks, block, width), BF16)
    normed, packed = pl.pallas_call(
        normalize_and_pack,
        out_shape=(rows, buffer),
        grid_spec=pltpu.PrefetchScalarGridSpec(
            num_scalar_prefetch=1,
            grid=(1,),
            in_specs=[whole(*inflow.shape), whole(1, width)],
            out_specs=[whole(*rows.shape), whole(*buffer.shape)],
        ),
        compiler_params=pltpu.CompilerParams(vmem_limit_bytes=VMEM_BYTES),
    )(chosen, inflow, gain)
    arrived = lax.all_to_all(packed, "turb", split_axis=0, concat_axis=0, tiled=True)

    wkv = jnp.concatenate([key_weight, value_weight], axis=1)

    def sample_block(index):
        return pl.BlockSpec((1, block, width), lambda i, o, s, t, c: (o[i], 0, 0))

    def up_block(u):
        return pl.BlockSpec((1, block, width), lambda i, o, s, t, c: (s[UPSTREAM * i + u], 0, 0))

    layer_output, grad_own, sent, gw = pl.pallas_call(
        attend,
        out_shape=(
            rows,
            jax.ShapeDtypeStruct((samples, block, width), F32),
            buffer,
            jax.ShapeDtypeStruct((4, width, width), F32),
        ),
        grid_spec=pltpu.PrefetchScalarGridSpec(
            num_scalar_prefetch=4,
            grid=(samples,),
            in_specs=[sample_block(0)] * 3
            + [up_block(u) for u in range(UPSTREAM)]
            + [
                whole(width, width),
                whole(width, 2 * width),
                whole(2 * width, width),
                whole(width, width),
                whole(width, width),
                whole(width, width),
            ],
            out_specs=[
                sample_block(0),
                sample_block(0),
                whole(*buffer.shape),
                whole(4, width, width),
            ],
            scratch_shapes=[
                pltpu.VMEM(((1 + UPSTREAM) * block, width), BF16),
                pltpu.VMEM(((1 + UPSTREAM) * block, 2 * width), BF16),
                pltpu.VMEM((2 * width, (1 + UPSTREAM) * block), BF16),
                pltpu.VMEM(((1 + UPSTREAM) * block, 2 * width), BF16),
                pltpu.VMEM((width, block), BF16),
                pltpu.VMEM((width, block), BF16),
            ],
        ),
        compiler_params=pltpu.CompilerParams(vmem_limit_bytes=VMEM_BYTES),
    )(
        order,
        source,
        target,
        count,
        normed,
        inflow,
        cotangent,
        arrived,
        arrived,
        arrived,
        query_weight,
        wkv,
        wkv.T,
        query_weight.T,
        out_weight,
        out_weight.T,
    )
    returned = lax.all_to_all(sent, "turb", split_axis=0, concat_axis=0, tiled=True)
    grad_inflow = pl.pallas_call(
        finish,
        out_shape=rows,
        grid_spec=pltpu.PrefetchScalarGridSpec(
            num_scalar_prefetch=2,
            grid=(1,),
            in_specs=[
                whole(samples, block, width),
                whole(*buffer.shape),
                whole(*inflow.shape),
                whole(*inflow.shape),
                whole(1, width),
            ],
            out_specs=whole(*rows.shape),
            scratch_shapes=[pltpu.VMEM((samples, block, width), F32)],
        ),
        compiler_params=pltpu.CompilerParams(vmem_limit_bytes=VMEM_BYTES),
    )(chosen, wanted, grad_own, returned, inflow, cotangent, gain)
    gw = lax.psum(gw, ("sample", "turb"))
    weighted = (
        query_weight.astype(F32) * gw[0]
        + key_weight.astype(F32) * gw[1]
        + value_weight.astype(F32) * gw[2]
    )
    gain_grad = jnp.sum(weighted, axis=1) / norm_gain
    return (layer_output, grad_inflow, gw[0], gw[1], gw[2], gw[3], gain_grad)


def solution(mesh):
    placed = (
        P("sample", "turb", None),
        P("sample", "turb", None),
        P(),
        P(),
        P(),
        P(),
        P(),
        P(),
        P("sample"),
    )
    return jax.shard_map(
        on_device,
        mesh=mesh,
        in_specs=placed,
        out_specs=(P("sample", "turb", None), P("sample", "turb", None), P(), P(), P(), P(), P()),
        check_vma=False,
    )
```

```python
import jax
import jax.numpy as jnp
from jax import lax
from jax.experimental import pallas as pl
from jax.experimental.pallas import tpu as pltpu
from jax.sharding import PartitionSpec as P

F32 = jnp.float32
BF16 = jnp.bfloat16
HEADS = 8
UPSTREAM = 3
EPSILON = 1e-05
VMEM_BYTES = 56 << 20
MESH = pl.DeviceIdType.MESH
BACK = (1, 9, 15, 19, 23, 27)


def dot(a, b):
    return jnp.dot(a, b, preferred_element_type=F32)


def dot_nt(a, b):
    return lax.dot_general(a, b, (((1,), (1,)), ((), ())), preferred_element_type=F32)


def whole(*shape):
    return pl.BlockSpec(shape, lambda *_: (0,) * len(shape))


def row_statistics(rows):
    widened = rows.astype(F32)
    centred = widened - jnp.mean(widened, axis=-1, keepdims=True)
    inverse = lax.rsqrt(jnp.mean(centred * centred, axis=-1, keepdims=True) + EPSILON)
    return centred * inverse, inverse


def normalize_and_pack(chosen_ref, inflow_ref, gain_ref, normed_ref, packed_ref):
    for s in range(inflow_ref.shape[0]):
        scaled, _ = row_statistics(inflow_ref[s])
        normed_ref[s] = (scaled * gain_ref[...]).astype(BF16)

    @pl.loop(0, packed_ref.shape[0])
    def _(d):
        packed_ref[d] = normed_ref[chosen_ref[d]]


def attend(
    order_ref,
    source_ref,
    target_ref,
    count_ref,
    own_ref,
    inflow_ref,
    cotangent_ref,
    up0_ref,
    up1_ref,
    up2_ref,
    wq_ref,
    wkv_ref,
    wkv_t_ref,
    wq_t_ref,
    wo_ref,
    wo_t_ref,
    out_ref,
    grad_own_ref,
    sent_ref,
    gw_ref,
    x_ref,
    kv_ref,
    kvt_ref,
    dkv_ref,
    att_t_ref,
    dq_t_ref,
):
    step = pl.program_id(0)
    block, width = own_ref.shape[1], own_ref.shape[2]
    pair = 2 * (width // HEADS)
    used = count_ref[step]

    @pl.when(step == 0)
    def _():
        gw_ref[...] = jnp.zeros_like(gw_ref)

    own = own_ref[0]
    cot = cotangent_ref[0]
    x_ref[0:block] = own
    for u, ref in enumerate((up0_ref, up1_ref, up2_ref)):
        x_ref[(u + 1) * block : (u + 2) * block] = ref[0]
    x = x_ref[...]
    kv_ref[...] = dot(x, wkv_ref[...]).astype(BF16)
    kvt_ref[...] = dot_nt(wkv_t_ref[...], x).astype(BF16)
    queries = (dot(own, wq_ref[...]).astype(BF16).astype(F32) * 0.125).astype(BF16)
    grads = dot(cot, wo_t_ref[...]).astype(BF16)
    lane = lax.broadcasted_iota(jnp.int32, (block, pair), 1) < pair // 2
    sub = lax.broadcasted_iota(jnp.int32, (pair, block), 0) < pair // 2
    zero = jnp.zeros((block, pair), BF16)
    bias = [jnp.where(u < used, 0.0, -1e30).astype(F32) for u in range(UPSTREAM)]

    def spread(rows):
        return jnp.concatenate([jnp.where(lane, rows, zero), jnp.where(lane, zero, rows)], axis=0)

    for p in range(width // pair):
        lo, hi = p * pair, (p + 1) * pair
        q_pair = spread(queries[:, lo:hi])
        g_pair = spread(grads[:, lo:hi])
        scores = dot_nt(kv_ref[:, lo:hi], q_pair)
        scores = jnp.concatenate(
            [scores[0:block]]
            + [scores[(u + 1) * block : (u + 2) * block] + bias[u] for u in range(UPSTREAM)],
            axis=0,
        )
        highest = jnp.max(scores, axis=0, keepdims=True)
        weights = jnp.exp(scores - highest)
        probs = weights * (1.0 / jnp.sum(weights, axis=0, keepdims=True))
        rounded = probs.astype(BF16)
        grad_probs = dot_nt(kv_ref[:, width + lo : width + hi], g_pair)
        centre = jnp.sum(probs * grad_probs, axis=0, keepdims=True)
        grad_scores = (probs * (grad_probs - centre)).astype(BF16)
        dkv_ref[:, width + lo : width + hi] = dot(rounded, g_pair).astype(BF16)
        dkv_ref[:, lo:hi] = dot(grad_scores, q_pair).astype(BF16)
        both = dot(kvt_ref[width + lo : width + hi, :], rounded)
        att_t_ref[lo:hi, :] = jnp.where(sub, both[:, :block], both[:, block:]).astype(BF16)
        both = dot(kvt_ref[lo:hi, :], grad_scores) * 0.125
        dq_t_ref[lo:hi, :] = jnp.where(sub, both[:, :block], both[:, block:]).astype(BF16)

    attended = att_t_ref[...].T
    dq = dq_t_ref[...].T
    out_ref[0] = (inflow_ref[0].astype(F32) + dot(attended, wo_ref[...])).astype(BF16)
    back = dot(dkv_ref[...], wkv_t_ref[...])
    grad_own_ref[0] = back[0:block] + dot(dq, wq_t_ref[...])
    for u in range(UPSTREAM):
        sent_ref[target_ref[UPSTREAM * step + u]] = back[
            (u + 1) * block : (u + 2) * block
        ].astype(BF16)
    x_t = x.T
    gw_ref[0] += dot(x_t[:, 0:block], dq)
    gw_kv = dot(x_t, dkv_ref[...])
    gw_ref[1] += gw_kv[:, :width]
    gw_ref[2] += gw_kv[:, width:]
    gw_ref[3] += dot(att_t_ref[...], cot)


def finish(
    chosen_ref, wanted_ref, grad_own_ref, returned_ref, inflow_ref, cotangent_ref, gain_ref, out_ref, sum_ref
):
    sum_ref[...] = grad_own_ref[...]

    @pl.loop(0, returned_ref.shape[0])
    def _(d):
        @pl.when(wanted_ref[d] > 0)
        def _():
            s = chosen_ref[d]
            sum_ref[s] = sum_ref[s] + returned_ref[d].astype(F32)

    for s in range(inflow_ref.shape[0]):
        scaled, inverse = row_statistics(inflow_ref[s])
        grad_scaled = sum_ref[s] * gain_ref[...]
        grad_input = inverse * (
            grad_scaled
            - jnp.mean(grad_scaled, axis=-1, keepdims=True)
            - scaled * jnp.mean(grad_scaled * scaled, axis=-1, keepdims=True)
        )
        out_ref[s] = (cotangent_ref[s].astype(F32) + grad_input).astype(BF16)


def exchange(
    sent_ref,
    gw_ref,
    returned_ref,
    total_ref,
    half_ref,
    core_in_ref,
    a1_in_ref,
    b1_in_ref,
    a2_in_ref,
    b2_in_ref,
    a1_ref,
    b1_ref,
    last_ref,
    last_in_ref,
    local_sem,
    back_send,
    back_recv,
    core_send,
    core_recv,
    a_send,
    a_recv,
    b_send,
    b_recv,
):
    sample = lax.axis_index("sample")
    turb = lax.axis_index("turb")
    core = lax.rem(sample, 2)
    high = sample - core
    x, yz = turb // 8, lax.rem(turb, 8)
    half = half_ref.shape[0]
    x_rows, yz_rows, last_rows = a1_ref.shape[0], b1_ref.shape[0], last_ref.shape[0] // 2
    color = half // 2

    def at_turb(k):
        return {"turb": turb ^ k}

    partner = {"sample": high + 1 - core}
    across = {"sample": lax.rem(sample + 2, 4)}

    barrier = pltpu.get_barrier_semaphore()
    pl.semaphore_signal(barrier, inc=1, device_id=partner, device_id_type=MESH)
    pl.semaphore_signal(barrier, inc=1, device_id=across, device_id_type=MESH)

    @pl.loop(1, 32)
    def _(k):
        pl.semaphore_signal(barrier, inc=1, device_id=at_turb(k), device_id_type=MESH)

    pl.semaphore_wait(barrier, 33)

    def remote(source, target, send, recv, device):
        return pltpu.make_async_remote_copy(
            src_ref=source,
            dst_ref=target,
            send_sem=send,
            recv_sem=recv,
            device_id=device,
            device_id_type=MESH,
        )

    def back(k):
        return remote(
            sent_ref.at[turb ^ k], returned_ref.at[turb], back_send.at[k], back_recv.at[k], at_turb(k)
        )

    def start_back(low, high):
        @pl.loop(low, high)
        def _(k):
            back(k).start()

    def rows(ref, start, count):
        return ref.at[pl.ds(pl.multiple_of(start, 8), count)]

    def start_all(copies):
        for c in copies:
            c.start()

    def wait_all(copies):
        for c in copies:
            c.wait()

    own_half = pltpu.make_async_copy(rows(gw_ref, core * half, half), half_ref, local_sem.at[0])
    own_half.start()
    fold = remote(
        rows(gw_ref, (1 - core) * half, half), core_in_ref, core_send.at[0], core_recv.at[0], partner
    )
    fold.start()
    start_back(BACK[0], BACK[1])
    own_half.wait()
    fold.wait()
    half_ref[...] = half_ref[...] + core_in_ref[...]

    over_x = [
        remote(
            rows(half_ref, (x ^ k) * x_rows, x_rows),
            a1_in_ref.at[k],
            a_send.at[0, k],
            a_recv.at[0, k],
            at_turb(8 * k),
        )
        for k in range(1, 4)
    ]
    over_yz = [
        remote(
            rows(half_ref, color + (yz ^ k) * yz_rows, yz_rows),
            b1_in_ref.at[k],
            b_send.at[0, k],
            b_recv.at[0, k],
            at_turb(k),
        )
        for k in range(1, 8)
    ]
    start_all(over_x + over_yz)
    start_back(BACK[1], BACK[2])
    wait_all(over_x)
    a1_ref[...] = (
        half_ref[pl.ds(pl.multiple_of(x * x_rows, 8), x_rows), :]
        + a1_in_ref[1]
        + a1_in_ref[2]
        + a1_in_ref[3]
    )
    second_a = [
        remote(
            rows(a1_ref, (yz ^ k) * last_rows, last_rows),
            a2_in_ref.at[k],
            a_send.at[1, k],
            a_recv.at[1, k],
            at_turb(k),
        )
        for k in range(1, 8)
    ]
    start_all(second_a)
    wait_all(over_yz)
    b1 = half_ref[pl.ds(pl.multiple_of(color + yz * yz_rows, 8), yz_rows), :]
    for k in range(1, 8):
        b1 = b1 + b1_in_ref[k]
    b1_ref[...] = b1
    second_b = [
        remote(
            rows(b1_ref, (x ^ k) * last_rows, last_rows),
            b2_in_ref.at[k],
            b_send.at[1, k],
            b_recv.at[1, k],
            at_turb(8 * k),
        )
        for k in range(1, 4)
    ]
    start_all(second_b)
    start_back(BACK[2], BACK[3])
    wait_all(second_a)
    a2 = a1_ref[pl.ds(pl.multiple_of(yz * last_rows, 8), last_rows), :]
    for k in range(1, 8):
        a2 = a2 + a2_in_ref[k]
    last_ref[0:last_rows] = a2
    wait_all(second_b)
    b2 = b1_ref[pl.ds(pl.multiple_of(x * last_rows, 8), last_rows), :]
    for k in range(1, 4):
        b2 = b2 + b2_in_ref[k]
    last_ref[last_rows : 2 * last_rows] = b2
    swap = remote(last_ref, last_in_ref, core_send.at[1], core_recv.at[1], across)
    swap.start()
    start_back(BACK[3], BACK[4])
    swap.wait()
    last_ref[...] = last_ref[...] + last_in_ref[...]

    a_row = core * half + x * x_rows
    b_row = core * half + color + yz * yz_rows
    a_last = rows(total_ref, a_row + yz * last_rows, last_rows)
    b_last = rows(total_ref, b_row + x * last_rows, last_rows)
    keep_a = pltpu.make_async_copy(last_ref.at[0:last_rows], a_last, local_sem.at[1])
    keep_b = pltpu.make_async_copy(last_ref.at[last_rows : 2 * last_rows], b_last, local_sem.at[2])
    gather_a = [
        remote(last_ref.at[0:last_rows], a_last, a_send.at[2, k], a_recv.at[2, k], at_turb(k))
        for k in range(1, 8)
    ]
    gather_b = [
        remote(
            last_ref.at[last_rows : 2 * last_rows],
            b_last,
            b_send.at[2, k],
            b_recv.at[2, k],
            at_turb(8 * k),
        )
        for k in range(1, 4)
    ]
    start_all([keep_a, keep_b] + gather_a + gather_b)
    start_back(BACK[4], BACK[5])
    wait_all([keep_a] + gather_a)
    a_part = rows(total_ref, a_row, x_rows)
    spread_a = [
        remote(a_part, a_part, a_send.at[3, k], a_recv.at[3, k], at_turb(8 * k)) for k in range(1, 4)
    ]
    start_all(spread_a)
    wait_all([keep_b] + gather_b)
    b_part = rows(total_ref, b_row, yz_rows)
    spread_b = [
        remote(b_part, b_part, b_send.at[3, k], b_recv.at[3, k], at_turb(k)) for k in range(1, 8)
    ]
    start_all(spread_b)
    start_back(BACK[5], 32)
    wait_all(spread_a)
    a_half = rows(total_ref, core * half, color)
    share_a = remote(a_half, a_half, core_send.at[2], core_recv.at[2], partner)
    share_a.start()
    wait_all(spread_b)
    b_half = rows(total_ref, core * half + color, color)
    share_b = remote(b_half, b_half, core_send.at[3], core_recv.at[3], partner)
    share_b.start()

    @pl.loop(1, 32)
    def _(k):
        back(k).wait()

    share_a.wait()
    share_b.wait()


def exchange_gradients(sent, gw):
    total_rows, width = gw.shape
    half = total_rows // 2
    x_rows, yz_rows, last_rows = half // 8, half // 16, half // 64
    anywhere = pl.BlockSpec(memory_space=pl.ANY)
    dma = pltpu.SemaphoreType.DMA
    return pl.pallas_call(
        exchange,
        out_shape=(
            jax.ShapeDtypeStruct(sent.shape, sent.dtype),
            jax.ShapeDtypeStruct(gw.shape, gw.dtype),
        ),
        in_specs=[anywhere, anywhere],
        out_specs=[anywhere, anywhere],
        scratch_shapes=[
            pltpu.VMEM((half, width), F32),
            pltpu.VMEM((half, width), F32),
            pltpu.VMEM((4, x_rows, width), F32),
            pltpu.VMEM((8, yz_rows, width), F32),
            pltpu.VMEM((8, last_rows, width), F32),
            pltpu.VMEM((4, last_rows, width), F32),
            pltpu.VMEM((x_rows, width), F32),
            pltpu.VMEM((yz_rows, width), F32),
            pltpu.VMEM((2 * last_rows, width), F32),
            pltpu.VMEM((2 * last_rows, width), F32),
            dma((3,)),
            dma((32,)),
            dma((32,)),
            dma((4,)),
            dma((4,)),
            dma((4, 8)),
            dma((4, 8)),
            dma((4, 8)),
            dma((4, 8)),
        ],
        compiler_params=pltpu.CompilerParams(
            vmem_limit_bytes=VMEM_BYTES, collective_id=0, has_side_effects=True
        ),
    )(sent, gw)


def on_device(
    inflow, cotangent, norm_gain, query_weight, key_weight, value_weight, out_weight, adjacency, sectors
):
    samples, block, width = inflow.shape
    blocks = lax.axis_size("turb")
    me = lax.axis_index("turb")
    gain = norm_gain.reshape(1, width)
    sample_ids = lax.broadcasted_iota(jnp.int32, (samples, samples), 0)
    sector_ids = lax.broadcasted_iota(jnp.int32, (samples, samples), 1)
    order = jnp.sum(jnp.where(sectors[:, None] == sector_ids, sample_ids, 0), axis=0)
    lists_me = adjacency == me
    chosen = jnp.sum(jnp.where(lists_me, order[:, None, None], 0), axis=(0, 2))
    wanted = jnp.sum(lists_me.astype(jnp.int32), axis=(0, 2))
    own_lists = lax.dynamic_index_in_dim(adjacency, me, axis=1, keepdims=False)
    usable = own_lists >= 0
    count = jnp.sum(usable.astype(jnp.int32), axis=1)
    spare = jnp.where(me == 0, 1, 0)
    source = jnp.where(usable, own_lists, spare).reshape(-1)
    target = jnp.where(usable, own_lists, me).reshape(-1)

    rows = jax.ShapeDtypeStruct((samples, block, width), BF16)
    buffer = jax.ShapeDtypeStruct((blocks, block, width), BF16)
    normed, packed = pl.pallas_call(
        normalize_and_pack,
        out_shape=(rows, buffer),
        grid_spec=pltpu.PrefetchScalarGridSpec(
            num_scalar_prefetch=1,
            grid=(1,),
            in_specs=[whole(*inflow.shape), whole(1, width)],
            out_specs=[whole(*rows.shape), whole(*buffer.shape)],
        ),
        compiler_params=pltpu.CompilerParams(vmem_limit_bytes=VMEM_BYTES),
    )(chosen, inflow, gain)
    arrived = lax.all_to_all(packed, "turb", split_axis=0, concat_axis=0, tiled=True)

    wkv = jnp.concatenate([key_weight, value_weight], axis=1)

    def sample_block(index):
        return pl.BlockSpec((1, block, width), lambda i, o, s, t, c: (o[i], 0, 0))

    def up_block(u):
        return pl.BlockSpec((1, block, width), lambda i, o, s, t, c: (s[UPSTREAM * i + u], 0, 0))

    layer_output, grad_own, sent, gw = pl.pallas_call(
        attend,
        out_shape=(
            rows,
            jax.ShapeDtypeStruct((samples, block, width), F32),
            buffer,
            jax.ShapeDtypeStruct((4, width, width), F32),
        ),
        grid_spec=pltpu.PrefetchScalarGridSpec(
            num_scalar_prefetch=4,
            grid=(samples,),
            in_specs=[sample_block(0)] * 3
            + [up_block(u) for u in range(UPSTREAM)]
            + [
                whole(width, width),
                whole(width, 2 * width),
                whole(2 * width, width),
                whole(width, width),
                whole(width, width),
                whole(width, width),
            ],
            out_specs=[
                sample_block(0),
                sample_block(0),
                whole(*buffer.shape),
                whole(4, width, width),
            ],
            scratch_shapes=[
                pltpu.VMEM(((1 + UPSTREAM) * block, width), BF16),
                pltpu.VMEM(((1 + UPSTREAM) * block, 2 * width), BF16),
                pltpu.VMEM((2 * width, (1 + UPSTREAM) * block), BF16),
                pltpu.VMEM(((1 + UPSTREAM) * block, 2 * width), BF16),
                pltpu.VMEM((width, block), BF16),
                pltpu.VMEM((width, block), BF16),
            ],
        ),
        compiler_params=pltpu.CompilerParams(vmem_limit_bytes=VMEM_BYTES),
    )(
        order,
        source,
        target,
        count,
        normed,
        inflow,
        cotangent,
        arrived,
        arrived,
        arrived,
        query_weight,
        wkv,
        wkv.T,
        query_weight.T,
        out_weight,
        out_weight.T,
    )
    returned, gw = exchange_gradients(sent, gw.reshape(4 * width, width))
    grad_inflow = pl.pallas_call(
        finish,
        out_shape=rows,
        grid_spec=pltpu.PrefetchScalarGridSpec(
            num_scalar_prefetch=2,
            grid=(1,),
            in_specs=[
                whole(samples, block, width),
                whole(*buffer.shape),
                whole(*inflow.shape),
                whole(*inflow.shape),
                whole(1, width),
            ],
            out_specs=whole(*rows.shape),
            scratch_shapes=[pltpu.VMEM((samples, block, width), F32)],
        ),
        compiler_params=pltpu.CompilerParams(vmem_limit_bytes=VMEM_BYTES),
    )(chosen, wanted, grad_own, returned, inflow, cotangent, gain)
    gw = gw.reshape(4, width, width)
    weighted = (
        query_weight.astype(F32) * gw[0]
        + key_weight.astype(F32) * gw[1]
        + value_weight.astype(F32) * gw[2]
    )
    gain_grad = jnp.sum(weighted, axis=1) / norm_gain
    return (layer_output, grad_inflow, gw[0], gw[1], gw[2], gw[3], gain_grad)


def solution(mesh):
    placed = (
        P("sample", "turb", None),
        P("sample", "turb", None),
        P(),
        P(),
        P(),
        P(),
        P(),
        P(),
        P("sample"),
    )
    return jax.shard_map(
        on_device,
        mesh=mesh,
        in_specs=placed,
        out_specs=(P("sample", "turb", None), P("sample", "turb", None), P(), P(), P(), P(), P()),
        check_vma=False,
    )
```
